32 devices in a mesh: tm: 8 (over z, y), roll: 4 (over x, core).
Axes of the slice: x: 2, y: 2, z: 4, core: 2. Of those that a mesh axis runs over, the one named last changes fastest.
Arguments:
- inputs: bfloat16 [4, 64, 32, 2048], P('roll', 'tm'), may hold values from -30 to 30
- cotangent: bfloat16 [4, 64, 32, 2048], P('roll', 'tm'), may hold values from -6 to 6
- memory_lists: int32 [4, 64, 8], P('roll', 'tm'), may hold values from -1 to 55, as said below
- w_query: bfloat16 [2048, 1024], replicated, may hold values from -1 to 1
- w_key: bfloat16 [2048, 1024], replicated, may hold values from -1 to 1
- w_value: bfloat16 [2048, 1024], replicated, may hold values from -0.125 to 0.125
- w_output: bfloat16 [1024, 2048], replicated, may hold values from -0.1875 to 0.1875
Outputs:
- attended: bfloat16 [4, 64, 32, 2048], P('roll', 'tm')
- grad_input: bfloat16 [4, 64, 32, 2048], P('roll', 'tm')
- grad_w_query: float32 [2048, 1024], P('tm')
- grad_w_key: float32 [2048, 1024], P('tm')
- grad_w_value: float32 [2048, 1024], P('tm')
- grad_w_output: float32 [1024, 2048], P('tm')
The draws below stay inside these ranges and needn't reach their ends.
Inputs may be any that keep to these rules, and one draw needn't show every extreme that they name: `memory_lists`: every entry is -1 or a frame of the same rollout that lies in an earlier block of 8 frames and before frame f - 4. The frames named in one list differ, and -1 entries come after them. The frames of one block name at most 3 distinct frames of any other block, and exactly 3 of the block just before theirs.
All inputs are finite; a program needn't handle non-finite values.
Results may differ from the reference program's by a relative error of at most 0.02.
Values may be sent and summed in bfloat16 or wider, within the bound.
A program may use at most 192 MiB of HBM per device.

```python
import jax
import jax.numpy as jnp
from jax import lax

D = 2048
HEADS = 8
HEAD = 128
TPF = 32
BAND = 4
MEM = 8
CAP = 3
FR_DEV = 8
HD = 1024
FRAMES = 64
ROLLOUTS = 4
N_TM = 8


def draw_inputs(key, part):
    normal_rows = jax.random.normal(jax.random.fold_in(key, 3), (ROLLOUTS, FRAMES, TPF, D), jnp.float32)
    normal_rows = jnp.clip(normal_rows, -6.0, 6.0)
    return normal_rows.astype(jnp.bfloat16)


def projection_pair(key):
    former = jnp.clip(jax.random.normal(jax.random.fold_in(key, 21), (D, HD), jnp.float32), -4.0, 4.0)
    latter = jnp.clip(jax.random.normal(jax.random.fold_in(key, 22), (D, HD), jnp.float32), -4.0, 4.0)
    return (former * D ** (-0.5), latter * D ** (-0.5))


def draw_w_query(key, part):
    former, latter = projection_pair(key)
    return former.astype(jnp.bfloat16)


def draw_w_key(key, part):
    former, latter = projection_pair(key)
    blended = latter
    return blended.astype(jnp.bfloat16)


def one_rollout(key):
    blocks = FRAMES // FR_DEV
    frame = jnp.arange(FRAMES, dtype=jnp.int32)
    block_of = frame // FR_DEV
    within = frame % FR_DEV
    noise = jax.random.randint(jax.random.fold_in(key, 31), (blocks, blocks, FR_DEV), 0, 4096) * FR_DEV
    noise = noise + jnp.arange(FR_DEV, dtype=jnp.int32)
    ordering = jnp.argsort(noise, axis=2)
    chosen = jnp.argsort(ordering, axis=2) < CAP
    allowed = chosen[block_of[:, None], block_of[None, :], within[None, :]]
    allowed = allowed & (block_of[None, :] < block_of[:, None]) & (frame[None, :] < frame[:, None] - BAND)
    forced = allowed & (block_of[None, :] == block_of[:, None] - 1) & (within[:, None] == FR_DEV - 1)
    ranking = jax.random.randint(jax.random.fold_in(key, 32), (FRAMES, FRAMES), 0, 65536) * FRAMES
    ranking = ranking + frame[None, :] + forced.astype(jnp.int32) * 2 ** 28
    ranking = jnp.where(allowed, ranking, -1)
    best, picked = lax.top_k(ranking, MEM)
    return jnp.where(best >= 0, picked, -1).astype(jnp.int32)


def draw_memory_lists(key, part):
    return jax.vmap(one_rollout)(jax.random.split(key, ROLLOUTS))


def block_levels(rng, dims, cuts, least, top_value):
    def one(position, parts):
        steps = jax.random.uniform(jax.random.fold_in(jax.random.fold_in(rng, 6), position), (parts,), jnp.float32, least / len(cuts), top_value / len(cuts))
        return jnp.repeat(jnp.exp(steps), dims[position] // parts).reshape((-1,) + (1,) * (len(dims) - position - 1))

    factor_of = one(*cuts[0])
    for cut in cuts[1:]:
        factor_of = factor_of * one(*cut)
    return factor_of


def scatter_about(rng, dims, width, most, cuts=(), held_as=jnp.bfloat16):
    result = jax.random.normal(rng, dims, jnp.float32) * width
    if len(cuts) > 0:
        result = block_levels(rng, dims, cuts, -0.22, 0.18) * result
    return jnp.clip(result, min=-most, max=most).astype(held_as)


def setup_inputs(seed: int = 0) -> dict:
    keys = jax.random.split(jax.random.key(seed), 8)
    return {
        "inputs": draw_inputs(jax.random.fold_in(keys[7], 71), 0),
        "cotangent": scatter_about(keys[1], (ROLLOUTS, FRAMES, TPF, D), 1.0, 6.0, ((0, 4), (1, 8))),
        "memory_lists": draw_memory_lists(jax.random.fold_in(keys[7], 71), 0),
        "w_query": draw_w_query(jax.random.fold_in(keys[7], 71), 0),
        "w_key": draw_w_key(jax.random.fold_in(keys[7], 71), 0),
        "w_value": scatter_about(keys[5], (D, HD), D ** -0.5, 0.125),
        "w_output": scatter_about(keys[6], (HD, D), HD ** -0.5, 0.1875),
    }


masked_score = -1e30


def to_half(values):
    return lax.optimization_barrier(values.astype(jnp.bfloat16))


def widen(values):
    return values.astype(jnp.float32)


def dot_last(left, right):
    return lax.dot_general(left, right, (((1,), (1,)), ((), ())), preferred_element_type=jnp.float32)


def dot_first(left, right):
    return lax.dot_general(left, right, (((0,), (0,)), ((), ())), preferred_element_type=jnp.float32)


def attend(queries, keyset, key_valid, grad_heads):
    frame_count, key_count, frame_tokens, double_width = keyset.shape
    inner_width = double_width // 2
    score_scale = HEAD ** -0.5
    query_f = widen(queries).reshape(frame_count, frame_tokens, HEADS, HEAD)
    key_f = widen(keyset[..., :inner_width]).reshape(frame_count, key_count * frame_tokens, HEADS, HEAD)
    value_f = widen(keyset[..., inner_width:]).reshape(frame_count, key_count * frame_tokens, HEADS, HEAD)
    grad_f = widen(grad_heads).reshape(frame_count, frame_tokens, HEADS, HEAD)
    scores = jnp.einsum("fqhe,fkhe->fhqk", query_f, key_f) * score_scale
    key_mask = jnp.repeat(key_valid, frame_tokens, axis=1)[:, None, None, :]
    scores = jnp.where(key_mask, scores, masked_score)
    row_max = jnp.max(scores, axis=-1, keepdims=True)
    weights = jnp.exp(scores - row_max)
    weights = weights / jnp.sum(weights, axis=-1, keepdims=True)
    rounded = widen(to_half(weights))
    heads_out = to_half(jnp.einsum("fhqk,fkhe->fqhe", rounded, value_f))
    grad_prob = jnp.einsum("fqhe,fkhe->fhqk", grad_f, value_f)
    row_dot = jnp.sum(weights * grad_prob, axis=-1, keepdims=True)
    dscore = widen(to_half(weights * (grad_prob - row_dot)))
    grad_query = to_half(jnp.einsum("fhqk,fkhe->fqhe", dscore, key_f) * score_scale)
    grad_keys = jnp.einsum("fhqk,fqhe->fkhe", dscore, query_f) * score_scale
    grad_values = jnp.einsum("fhqk,fqhe->fkhe", rounded, grad_f)
    block_shape = (frame_count, key_count, frame_tokens, inner_width)
    grad_keyval = jnp.concatenate([grad_keys.reshape(block_shape), grad_values.reshape(block_shape)], axis=-1)
    return (heads_out.reshape(frame_count, frame_tokens, inner_width),
            grad_query.reshape(frame_count, frame_tokens, inner_width), grad_keyval)


def rollout_pass(inputs, cotangent, recalled, w_query, w_key, w_value, w_output):
    row_count = FRAMES * TPF
    flat_input = inputs.reshape(row_count, D)
    grad_flat = cotangent.reshape(row_count, D)
    queries = to_half(jnp.dot(flat_input, w_query, preferred_element_type=jnp.float32)).reshape(FRAMES, TPF, HD)
    key_rows = to_half(jnp.dot(flat_input, w_key, preferred_element_type=jnp.float32))
    value_rows = to_half(jnp.dot(flat_input, w_value, preferred_element_type=jnp.float32))
    keyval = jnp.concatenate([key_rows, value_rows], axis=1).reshape(FRAMES, TPF, 2 * HD)
    grad_heads = to_half(dot_last(grad_flat, w_output)).reshape(FRAMES, TPF, HD)
    offsets = jnp.arange(BAND + 1, dtype=jnp.int32) - BAND

    def one_block(running, block_index):
        first_frame = (block_index * FR_DEV).astype(jnp.int32)
        frame_ids = first_frame + jnp.arange(FR_DEV, dtype=jnp.int32)
        band_ids = frame_ids[:, None] + offsets[None, :]
        memory_ids = lax.dynamic_slice_in_dim(recalled, first_frame, FR_DEV, 0).astype(jnp.int32)
        all_ids = jnp.concatenate([band_ids, memory_ids], axis=1)
        key_valid = all_ids >= 0
        safe_ids = jnp.where(key_valid, all_ids, 0).astype(jnp.int32)
        keyset = keyval[safe_ids]
        block_queries = lax.dynamic_slice_in_dim(queries, first_frame, FR_DEV, 0)
        block_grads = lax.dynamic_slice_in_dim(grad_heads, first_frame, FR_DEV, 0)
        heads_out, grad_query, grad_keyval = attend(block_queries, keyset, key_valid, block_grads)
        band_part = grad_keyval[:, :BAND + 1].reshape(FR_DEV * (BAND + 1), TPF, 2 * HD)
        band_target = safe_ids[:, :BAND + 1].reshape(-1)
        own_mask = (band_target >= first_frame)[:, None, None]
        own_sum = jax.ops.segment_sum(jnp.where(own_mask, band_part, 0.0), band_target, FRAMES)
        prev_sum = jax.ops.segment_sum(jnp.where(own_mask, 0.0, band_part), band_target, FRAMES)
        memory_part = grad_keyval[:, BAND + 1:].reshape(FR_DEV * MEM, TPF, 2 * HD)
        memory_sum = jax.ops.segment_sum(memory_part, safe_ids[:, BAND + 1:].reshape(-1), FRAMES)
        running = running + own_sum + widen(to_half(prev_sum)) + widen(to_half(memory_sum))
        return running, (heads_out, grad_query)

    start = jnp.zeros((FRAMES, TPF, 2 * HD), jnp.float32)
    summed, (outs, grads) = lax.scan(one_block, start, jnp.arange(N_TM, dtype=jnp.int32))
    keyval_grad = to_half(summed)
    heads_rows = outs.reshape(row_count, HD)
    grad_query = grads.reshape(row_count, HD)
    grad_keys = keyval_grad[..., :HD].reshape(row_count, HD)
    grad_values = keyval_grad[..., HD:].reshape(row_count, HD)
    grad_input = to_half(dot_last(grad_query, w_query) + dot_last(grad_keys, w_key) + dot_last(grad_values, w_value))
    attended = to_half(jnp.dot(heads_rows, w_output, preferred_element_type=jnp.float32))
    rows_block = FR_DEV * TPF

    def block_grads(running, pieces):
        piece_input, piece_query, piece_keys, piece_values, piece_heads, piece_grad = pieces
        partials = (dot_first(piece_input, piece_query), dot_first(piece_input, piece_keys),
                    dot_first(piece_input, piece_values), dot_first(piece_heads, piece_grad))
        return tuple(total + widen(to_half(term)) for total, term in zip(running, partials)), None

    zero_in = jnp.zeros((D, HD), jnp.float32)
    zero_out = jnp.zeros((HD, D), jnp.float32)
    stacked = (flat_input.reshape(N_TM, rows_block, D), grad_query.reshape(N_TM, rows_block, HD),
               grad_keys.reshape(N_TM, rows_block, HD), grad_values.reshape(N_TM, rows_block, HD),
               heads_rows.reshape(N_TM, rows_block, HD), grad_flat.reshape(N_TM, rows_block, D))
    weight_grads, unused = lax.scan(block_grads, (zero_in, zero_in, zero_in, zero_out), stacked)
    return (attended.reshape(FRAMES, TPF, D), grad_input.reshape(FRAMES, TPF, D), weight_grads)


def reference(inputs, cotangent, memory_lists, w_query, w_key, w_value, w_output):
    zero_in = jnp.zeros((D, HD), jnp.float32)
    zero_out = jnp.zeros((HD, D), jnp.float32)

    def per_rollout(running, pieces):
        piece_input, piece_grad, recalled = pieces
        attended, grad_input, weight_grads = rollout_pass(piece_input, piece_grad, recalled,
                                                          w_query, w_key, w_value, w_output)
        return tuple(total + term for total, term in zip(running, weight_grads)), (attended, grad_input)

    totals, (attended, grad_input) = lax.scan(per_rollout, (zero_in, zero_in, zero_in, zero_out),
                                              (inputs, cotangent, memory_lists))
    return attended, grad_input, totals[0], totals[1], totals[2], totals[3]
```

```python
import functools

import jax
import jax.numpy as jnp
from jax import lax
from jax.experimental import pallas as pl
from jax.experimental.pallas import tpu as pltpu
from jax.sharding import PartitionSpec as P

HEADS = 8
HEAD = 128
BAND = 4
MEM = 8
CAP = 3


masked_score = -1e30


def from_behind(block, axis, distance):
    devices = range(lax.axis_size(axis))
    route = [(i - distance, i) for i in devices if i - distance in devices]
    return lax.ppermute(block, axis, route)


def dot_last(left, right):
    return lax.dot_general(
        left, right, (((1,), (1,)), ((), ())), preferred_element_type=jnp.float32
    )


def dot_first(left, right):
    return lax.dot_general(
        left, right, (((0,), (0,)), ((), ())), preferred_element_type=jnp.float32
    )


def attend_kernel(q_ref, g_ref, ko_ref, vo_ref, kb_ref, vb_ref, ks_ref, vs_ref, bias_ref,
                  out_ref, gq_ref, gko_ref, gvo_ref, gkb_ref, gvb_ref, gks_ref, gvs_ref):
    scale = HEAD ** (-0.5)
    q = q_ref[...]
    g = g_ref[...]
    k = jnp.concatenate([ko_ref[...], kb_ref[...], ks_ref[...]], axis=0)
    v = jnp.concatenate([vo_ref[...], vb_ref[...], vs_ref[...]], axis=0)
    scores = dot_last(q, k) * scale + bias_ref[...]
    weights = jnp.exp(scores - jnp.max(scores, axis=-1, keepdims=True))
    weights = weights * (1.0 / jnp.sum(weights, axis=-1, keepdims=True))
    rounded = weights.astype(jnp.bfloat16)
    out_ref[...] = jnp.dot(rounded, v, preferred_element_type=jnp.float32).astype(jnp.bfloat16)
    grad_prob = dot_last(g, v)
    row_dot = jnp.sum(weights * grad_prob, axis=-1, keepdims=True)
    dscore = (weights * (grad_prob - row_dot)).astype(jnp.bfloat16)
    gq = jnp.dot(dscore, k, preferred_element_type=jnp.float32) * scale
    gq_ref[...] = gq.astype(jnp.bfloat16)
    gk = dot_first(dscore, q) * scale
    gv = dot_first(rounded, g)
    own = ko_ref.shape[0]
    ext = own + kb_ref.shape[0]
    gko_ref[...] = gk[:own]
    gvo_ref[...] = gv[:own]
    gkb_ref[...] = gk[own:ext].astype(jnp.bfloat16)
    gvb_ref[...] = gv[own:ext].astype(jnp.bfloat16)
    gks_ref[...] = gk[ext:].astype(jnp.bfloat16)
    gvs_ref[...] = gv[ext:].astype(jnp.bfloat16)


def attend(queries, grad_heads, key_own, value_own, before, slots, bias):
    rows, width = queries.shape
    heads = width // HEAD

    def column(count, shift=0):
        return pl.BlockSpec((count, HEAD), lambda h: (0, h + shift))

    nb, ns = before.shape[0], slots.shape[0]
    pool = rows + nb + ns
    half = jnp.bfloat16
    return pl.pallas_call(
        attend_kernel,
        grid=(heads,),
        in_specs=[
            column(rows), column(rows), column(rows), column(rows),
            column(nb), column(nb, heads), column(ns), column(ns, heads),
            pl.BlockSpec((rows, pool), lambda h: (0, 0)),
        ],
        out_specs=[
            column(rows), column(rows), column(rows), column(rows),
            column(nb), column(nb), column(ns), column(ns),
        ],
        out_shape=[
            jax.ShapeDtypeStruct((rows, width), half),
            jax.ShapeDtypeStruct((rows, width), half),
            jax.ShapeDtypeStruct((rows, width), jnp.float32),
            jax.ShapeDtypeStruct((rows, width), jnp.float32),
            jax.ShapeDtypeStruct((nb, width), half),
            jax.ShapeDtypeStruct((nb, width), half),
            jax.ShapeDtypeStruct((ns, width), half),
            jax.ShapeDtypeStruct((ns, width), half),
        ],
        compiler_params=pltpu.CompilerParams(vmem_limit_bytes=56 * 2**20),
        cost_estimate=pl.CostEstimate(
            flops=12 * rows * pool * width,
            bytes_accessed=8 * pool * width,
            transcendentals=heads * rows * pool,
        ),
        name="attend",
    )(queries, grad_heads, key_own, value_own, before, before, slots, slots, bias)


def toggled(value, mask, bit):
    k = 0
    while (1 << k) <= mask:
        if (mask >> k) & 1:
            step = 1 << k
            value = value + bit * step * (1 - 2 * ((value // step) % 2))
        k += 1
    return value


def masks_of(size):
    masks = []
    k = 0
    while (1 << k) < size:
        masks.append((1 << k) if k < 2 else (1 << k) + (1 << (k - 1)))
        k += 1
    return masks


def reduce_kernel(n_tm, n_roll, *refs):
    mats = 4
    parts, refs = refs[:mats], refs[mats:]
    outs, refs = refs[:mats], refs[mats:]
    own, refs = refs[:mats], refs[mats:]
    near, refs = refs[:mats], refs[mats:]
    far, refs = refs[:mats], refs[mats:]
    local_sem, near_send, near_recv, far_send, far_recv, share_send, share_recv = refs

    me_tm = lax.axis_index("tm")
    me_roll = lax.axis_index("roll")
    pair = ("roll", 1)
    roll_rest = [("roll", m) for m in masks_of(n_roll)[1:]]
    others = roll_rest + [("tm", m) for m in masks_of(n_tm)]
    count = len(others)
    kept = 1 << count

    def peer(direction):
        axis, mask = direction
        mine = me_tm if axis == "tm" else me_roll
        return {axis: toggled(mine, mask, 1)}

    barrier = pltpu.get_barrier_semaphore()
    for direction in [pair] + others:
        pl.semaphore_signal(
            barrier, inc=1, device_id=peer(direction), device_id_type=pl.DeviceIdType.MESH
        )
    pl.semaphore_wait(barrier, 1 + count)

    def order(m):
        shift = m % count
        return others[shift:] + others[:shift]

    def block_of(m, position, flip):
        tm, roll = me_tm, toggled(me_roll, 1, flip)
        for i, (axis, mask) in enumerate(order(m)):
            bit = (position // (1 << (count - 1 - i))) % 2
            if axis == "tm":
                tm = toggled(tm, mask, bit)
            else:
                roll = toggled(roll, mask, bit)
        return tm * n_roll + roll

    def near_copy(m, source, target):
        return pltpu.make_async_remote_copy(
            src_ref=source, dst_ref=target, send_sem=near_send.at[m], recv_sem=near_recv.at[m],
            device_id=peer(pair), device_id_type=pl.DeviceIdType.MESH,
        )

    def far_copy(m, s):
        size = kept >> (s + 1)
        return pltpu.make_async_remote_copy(
            src_ref=own[m].at[pl.ds(size, size)],
            dst_ref=far[m].at[pl.ds(size, size)],
            send_sem=far_send.at[m, s], recv_sem=far_recv.at[m, s],
            device_id=peer(order(m)[s]), device_id_type=pl.DeviceIdType.MESH,
        )

    for m in range(mats):
        @pl.loop(0, kept)
        def _(position):
            near_copy(m, parts[m].at[block_of(m, position, 1)], near[m].at[position]).start()
            pltpu.make_async_copy(
                parts[m].at[block_of(m, position, 0)], own[m].at[position], local_sem.at[m]
            ).start()

    def add(target, source, length, offset):
        @pl.loop(0, length)
        def _(i):
            total = target[i].astype(jnp.float32) + source[i + offset].astype(jnp.float32)
            target[i] = total.astype(jnp.bfloat16)

    for m in range(mats):
        whole = parts[m].at[pl.ds(0, kept)]
        pltpu.make_async_copy(whole, own[m], local_sem.at[m]).wait()
        near_copy(m, whole, near[m]).wait()
        add(own[m], near[m], kept, 0)
        far_copy(m, 0).start()

    for s in range(count):
        for m in range(mats):
            far_copy(m, s).wait()
            size = kept >> (s + 1)
            add(own[m], far[m], size, size)
            if s + 1 < count:
                far_copy(m, s + 1).start()

    for m in range(mats):
        outs[m][me_roll] = own[m][0]
    held = [0]
    index = 0
    for direction in roll_rest[::-1] + [pair]:
        def share(m, j, code):
            spot = outs[m].at[toggled_all(me_roll, code)]
            return pltpu.make_async_remote_copy(
                src_ref=spot, dst_ref=spot,
                send_sem=share_send.at[m, index + j], recv_sem=share_recv.at[m, index + j],
                device_id=peer(direction), device_id_type=pl.DeviceIdType.MESH,
            )

        for m in range(mats):
            for j, code in enumerate(held):
                share(m, j, code).start()
        for m in range(mats):
            for j, code in enumerate(held):
                share(m, j, code).wait()
        index += len(held)
        held = held + [code ^ direction[1] for code in held]


def toggled_all(value, code):
    return toggled(value, code, 1) if code else value


def reduce_all(parts, n_tm, n_roll):
    blocks = n_tm * n_roll
    kept = blocks // 2
    count = kept.bit_length() - 1
    shapes = [(p.shape[0] // blocks, p.shape[1]) for p in parts]
    half = jnp.bfloat16
    cubes = [p.reshape((blocks,) + s) for p, s in zip(parts, shapes)]
    sem = pltpu.SemaphoreType.DMA
    outs = pl.pallas_call(
        functools.partial(reduce_kernel, n_tm, n_roll),
        out_shape=[jax.ShapeDtypeStruct((n_roll,) + s, half) for s in shapes],
        in_specs=[pl.BlockSpec(memory_space=pl.ANY)] * 4,
        out_specs=[pl.BlockSpec(memory_space=pltpu.VMEM)] * 4,
        scratch_shapes=[pltpu.VMEM((kept,) + s, half) for s in shapes] * 3
        + [
            sem((4,)), sem((4,)), sem((4,)), sem((4, count)), sem((4, count)),
            sem((4, n_roll)), sem((4, n_roll)),
        ],
        compiler_params=pltpu.CompilerParams(
            collective_id=0, has_side_effects=True, vmem_limit_bytes=56 * 2**20
        ),
        name="reduce_all",
    )(*cubes)
    return [o.reshape(o.shape[0] * o.shape[1], o.shape[2]) for o in outs]


def local(inputs, cotangent, memory_lists, w_query, w_key, w_value, w_output):
    frame_count, frame_tokens, model_width = inputs.shape[1:]
    inner_width = w_query.shape[1]
    blocks = lax.axis_size("tm")
    position = lax.axis_index("tm")
    row_count = frame_count * frame_tokens
    flat_input = inputs.reshape(row_count, model_width)
    grad_flat = cotangent.reshape(row_count, model_width)
    queries = jnp.dot(flat_input, w_query, preferred_element_type=jnp.float32).astype(jnp.bfloat16)
    key_rows = jnp.dot(flat_input, w_key, preferred_element_type=jnp.float32).astype(jnp.bfloat16)
    value_rows = jnp.dot(flat_input, w_value, preferred_element_type=jnp.float32).astype(
        jnp.bfloat16
    )
    grad_heads = dot_last(grad_flat, w_output).astype(jnp.bfloat16)
    recalled = memory_lists[0]
    first_frame = position * frame_count
    last_rows = BAND * frame_tokens
    last_frames = jnp.concatenate(
        [key_rows[row_count - last_rows :], value_rows[row_count - last_rows :]], axis=-1
    )
    before = from_behind(last_frames, "tm", 1)
    all_lists = lax.all_gather(recalled, "tm", axis=0, tiled=True)
    targets = jnp.arange(blocks * frame_count, dtype=jnp.int32)
    wanted = jnp.any(recalled.reshape(-1, 1) == targets[None, :], axis=0).reshape(
        blocks, frame_count
    )
    slot_rank = jnp.cumsum(wanted.astype(jnp.int32), axis=1) - 1
    mem_ok = recalled >= 0
    slot_frame = jnp.where(
        wanted[:, None, :] & (slot_rank[:, None, :] == jnp.arange(CAP, dtype=jnp.int32)[:, None]),
        targets.reshape(blocks, 1, frame_count) + 1,
        0,
    ).sum(axis=-1).reshape(-1) - 1
    slot_ok = jnp.any(
        mem_ok[:, :, None] & (recalled[:, :, None] == slot_frame[None, None, :]), axis=1
    )
    pool_frame = first_frame + jnp.concatenate(
        [jnp.arange(frame_count, dtype=jnp.int32), jnp.arange(-BAND, 0, dtype=jnp.int32)]
    )
    ahead = (first_frame + jnp.arange(frame_count, dtype=jnp.int32))[:, None] - pool_frame[None, :]
    band_ok = (ahead >= 0) & (ahead <= BAND) & (pool_frame >= 0)[None, :]
    frame_ok = jnp.concatenate([band_ok, slot_ok], axis=1)
    bias = jnp.where(frame_ok, 0.0, masked_score).astype(jnp.float32)
    bias = jnp.repeat(jnp.repeat(bias, frame_tokens, axis=0), frame_tokens, axis=1)
    own_frames = first_frame + jnp.arange(frame_count, dtype=jnp.int32)
    requested = jnp.any(
        all_lists.reshape(blocks, frame_count * MEM, 1) == own_frames[None, None, :], axis=1
    )
    asked_rank = jnp.cumsum(requested.astype(jnp.int32), axis=1) - 1
    picker = requested[:, None, :] & (
        asked_rank[:, None, :] == jnp.arange(CAP, dtype=jnp.int32)[None, :, None]
    )
    picker = picker.astype(jnp.bfloat16)
    out_keys = jnp.einsum(
        "bcp,pz->bcz", picker, key_rows.reshape(frame_count, -1), preferred_element_type=jnp.float32
    )
    out_values = jnp.einsum(
        "bcp,pz->bcz",
        picker,
        value_rows.reshape(frame_count, -1),
        preferred_element_type=jnp.float32,
    )
    piece_shape = (blocks, CAP, frame_tokens, inner_width)
    outgoing = jnp.concatenate(
        [
            out_keys.astype(jnp.bfloat16).reshape(piece_shape),
            out_values.astype(jnp.bfloat16).reshape(piece_shape),
        ],
        axis=-1,
    )
    incoming = lax.all_to_all(outgoing, "tm", split_axis=0, concat_axis=0, tiled=True)
    slot_rows = incoming.reshape(blocks * CAP * frame_tokens, 2 * inner_width)
    (
        heads_rows, query_rows, own_keys, own_values, rim_keys, rim_values, slot_keys, slot_values
    ) = attend(queries, grad_heads, key_rows, value_rows, before, slot_rows, bias)
    rim = jnp.concatenate([rim_keys, rim_values], axis=-1)
    passed = from_behind(rim, "tm", -1)
    passed_full = jnp.pad(passed.astype(jnp.float32), ((row_count - last_rows, 0), (0, 0)))
    slot_grad = jnp.concatenate([slot_keys, slot_values], axis=-1).reshape(piece_shape[:3] + (-1,))
    returned = lax.all_to_all(slot_grad, "tm", split_axis=0, concat_axis=0, tiled=True)
    gathered_back = jnp.einsum(
        "bcp,bcz->pz", picker, returned.reshape(blocks, CAP, -1), preferred_element_type=jnp.float32
    )
    gathered_back = gathered_back.reshape(row_count, 2 * inner_width)
    grad_keys = (
        own_keys + passed_full[..., :inner_width] + gathered_back[..., :inner_width]
    ).astype(jnp.bfloat16)
    grad_values = (
        own_values + passed_full[..., inner_width:] + gathered_back[..., inner_width:]
    ).astype(jnp.bfloat16)
    grad_input = (
        dot_last(query_rows, w_query) + dot_last(grad_keys, w_key) + dot_last(grad_values, w_value)
    )
    grad_input = grad_input.astype(jnp.bfloat16).reshape(1, frame_count, frame_tokens, model_width)
    attended = jnp.dot(heads_rows, w_output, preferred_element_type=jnp.float32).astype(
        jnp.bfloat16
    )
    attended = attended.reshape(1, frame_count, frame_tokens, model_width)
    partials = (
        dot_first(flat_input, query_rows).astype(jnp.bfloat16),
        dot_first(flat_input, grad_keys).astype(jnp.bfloat16),
        dot_first(flat_input, grad_values).astype(jnp.bfloat16),
        dot_first(heads_rows, grad_flat).astype(jnp.bfloat16),
    )
    totals = [
        total.astype(jnp.float32)
        for total in reduce_all(partials, blocks, lax.axis_size("roll"))
    ]
    return (attended, grad_input, totals[0], totals[1], totals[2], totals[3])


def solution(mesh):
    return jax.shard_map(
        local,
        mesh=mesh,
        in_specs=(
            P("roll", "tm", None, None),
            P("roll", "tm", None, None),
            P("roll", "tm", None),
            P(),
            P(),
            P(),
            P(),
        ),
        out_specs=(
            P("roll", "tm", None, None),
            P("roll", "tm", None, None),
            P("tm", None),
            P("tm", None),
            P("tm", None),
            P("tm", None),
        ),
        check_vma=False,
    )
```

```python
import functools

import jax
import jax.numpy as jnp
from jax import lax
from jax.experimental import pallas as pl
from jax.experimental.pallas import tpu as pltpu
from jax.sharding import PartitionSpec as P

HEADS = 8
HEAD = 128
BAND = 4
MEM = 8
CAP = 3


masked_score = -1e30


def from_behind(block, axis, distance):
    devices = range(lax.axis_size(axis))
    route = [(i - distance, i) for i in devices if i - distance in devices]
    return lax.ppermute(block, axis, route)


def dot_last(left, right):
    return lax.dot_general(
        left, right, (((1,), (1,)), ((), ())), preferred_element_type=jnp.float32
    )


def dot_first(left, right):
    return lax.dot_general(
        left, right, (((0,), (0,)), ((), ())), preferred_element_type=jnp.float32
    )


def attend_kernel(q_ref, g_ref, ko_ref, vo_ref, kb_ref, vb_ref, ks_ref, vs_ref, bias_ref,
                  out_ref, gq_ref, gko_ref, gvo_ref, gkb_ref, gvb_ref, gks_ref, gvs_ref):
    scale = HEAD ** (-0.5)
    q = q_ref[...]
    g = g_ref[...]
    k = jnp.concatenate([ko_ref[...], kb_ref[...], ks_ref[...]], axis=0)
    v = jnp.concatenate([vo_ref[...], vb_ref[...], vs_ref[...]], axis=0)
    scores = dot_last(q, k) * scale + bias_ref[...]
    weights = jnp.exp(scores - jnp.max(scores, axis=-1, keepdims=True))
    weights = weights * (1.0 / jnp.sum(weights, axis=-1, keepdims=True))
    rounded = weights.astype(jnp.bfloat16)
    out_ref[...] = jnp.dot(rounded, v, preferred_element_type=jnp.float32).astype(jnp.bfloat16)
    grad_prob = dot_last(g, v)
    row_dot = jnp.sum(weights * grad_prob, axis=-1, keepdims=True)
    dscore = (weights * (grad_prob - row_dot)).astype(jnp.bfloat16)
    gq = jnp.dot(dscore, k, preferred_element_type=jnp.float32) * scale
    gq_ref[...] = gq.astype(jnp.bfloat16)
    gk = dot_first(dscore, q) * scale
    gv = dot_first(rounded, g)
    own = ko_ref.shape[0]
    ext = own + kb_ref.shape[0]
    gko_ref[...] = gk[:own]
    gvo_ref[...] = gv[:own]
    gkb_ref[...] = gk[own:ext].astype(jnp.bfloat16)
    gvb_ref[...] = gv[own:ext].astype(jnp.bfloat16)
    gks_ref[...] = gk[ext:].astype(jnp.bfloat16)
    gvs_ref[...] = gv[ext:].astype(jnp.bfloat16)


def attend(queries, grad_heads, key_own, value_own, before, slots, bias):
    rows, width = queries.shape
    heads = width // HEAD

    def column(count, shift=0):
        return pl.BlockSpec((count, HEAD), lambda h: (0, h + shift))

    nb, ns = before.shape[0], slots.shape[0]
    pool = rows + nb + ns
    half = jnp.bfloat16
    return pl.pallas_call(
        attend_kernel,
        grid=(heads,),
        in_specs=[
            column(rows), column(rows), column(rows), column(rows),
            column(nb), column(nb, heads), column(ns), column(ns, heads),
            pl.BlockSpec((rows, pool), lambda h: (0, 0)),
        ],
        out_specs=[
            column(rows), column(rows), column(rows), column(rows),
            column(nb), column(nb), column(ns), column(ns),
        ],
        out_shape=[
            jax.ShapeDtypeStruct((rows, width), half),
            jax.ShapeDtypeStruct((rows, width), half),
            jax.ShapeDtypeStruct((rows, width), jnp.float32),
            jax.ShapeDtypeStruct((rows, width), jnp.float32),
            jax.ShapeDtypeStruct((nb, width), half),
            jax.ShapeDtypeStruct((nb, width), half),
            jax.ShapeDtypeStruct((ns, width), half),
            jax.ShapeDtypeStruct((ns, width), half),
        ],
        compiler_params=pltpu.CompilerParams(vmem_limit_bytes=56 * 2**20),
        cost_estimate=pl.CostEstimate(
            flops=12 * rows * pool * width,
            bytes_accessed=8 * pool * width,
            transcendentals=heads * rows * pool,
        ),
        name="attend",
    )(queries, grad_heads, key_own, value_own, before, before, slots, slots, bias)


def toggled(value, mask, bit):
    k = 0
    while (1 << k) <= mask:
        if (mask >> k) & 1:
            step = 1 << k
            value = value + bit * step * (1 - 2 * ((value // step) % 2))
        k += 1
    return value


def masks_of(size):
    masks = []
    k = 0
    while (1 << k) < size:
        masks.append((1 << k) if k < 2 else (1 << k) + (1 << (k - 1)))
        k += 1
    return masks


def reduce_kernel(n_tm, n_roll, *refs):
    mats = 4
    parts, refs = refs[:mats], refs[mats:]
    outs, refs = refs[:mats], refs[mats:]
    own, refs = refs[:mats], refs[mats:]
    near, refs = refs[:mats], refs[mats:]
    far, refs = refs[:mats], refs[mats:]
    local_sem, near_send, near_recv, far_send, far_recv, share_send, share_recv = refs

    me_tm = lax.axis_index("tm")
    me_roll = lax.axis_index("roll")
    pair = ("roll", 1)
    roll_rest = [("roll", m) for m in masks_of(n_roll)[1:]]
    others = roll_rest + [("tm", m) for m in masks_of(n_tm)]
    count = len(others)
    kept = 1 << count

    def peer(direction):
        axis, mask = direction
        mine = me_tm if axis == "tm" else me_roll
        return {axis: toggled(mine, mask, 1)}

    barrier = pltpu.get_barrier_semaphore()
    for direction in [pair] + others:
        pl.semaphore_signal(
            barrier, inc=1, device_id=peer(direction), device_id_type=pl.DeviceIdType.MESH
        )
    pl.semaphore_wait(barrier, 1 + count)

    def order(m):
        shift = m % count
        return others[shift:] + others[:shift]

    def block_of(m, position, flip):
        tm, roll = me_tm, toggled(me_roll, 1, flip)
        for i, (axis, mask) in enumerate(order(m)):
            bit = (position // (1 << (count - 1 - i))) % 2
            if axis == "tm":
                tm = toggled(tm, mask, bit)
            else:
                roll = toggled(roll, mask, bit)
        return tm * n_roll + roll

    def near_copy(m, source, target):
        return pltpu.make_async_remote_copy(
            src_ref=source, dst_ref=target, send_sem=near_send.at[m], recv_sem=near_recv.at[m],
            device_id=peer(pair), device_id_type=pl.DeviceIdType.MESH,
        )

    def far_copy(m, s):
        size = kept >> (s + 1)
        return pltpu.make_async_remote_copy(
            src_ref=own[m].at[pl.ds(size, size)],
            dst_ref=far[m].at[pl.ds(size, size)],
            send_sem=far_send.at[m, s], recv_sem=far_recv.at[m, s],
            device_id=peer(order(m)[s]), device_id_type=pl.DeviceIdType.MESH,
        )

    for m in range(mats):
        @pl.loop(0, kept)
        def _(position):
            near_copy(m, parts[m].at[block_of(m, position, 1)], near[m].at[position]).start()
            pltpu.make_async_copy(
                parts[m].at[block_of(m, position, 0)], own[m].at[position], local_sem.at[m]
            ).start()

    def add(target, source, length, offset):
        @pl.loop(0, length)
        def _(i):
            total = target[i].astype(jnp.float32) + source[i + offset].astype(jnp.float32)
            target[i] = total.astype(jnp.bfloat16)

    for m in range(mats):
        whole = parts[m].at[pl.ds(0, kept)]
        pltpu.make_async_copy(whole, own[m], local_sem.at[m]).wait()
        near_copy(m, whole, near[m]).wait()
        add(own[m], near[m], kept, 0)
        far_copy(m, 0).start()

    for s in range(count):
        for m in range(mats):
            far_copy(m, s).wait()
            size = kept >> (s + 1)
            add(own[m], far[m], size, size)
            if s + 1 < count:
                far_copy(m, s + 1).start()

    for m in range(mats):
        outs[m][me_roll] = own[m][0]
    held = [0]
    index = 0
    for direction in roll_rest[::-1] + [pair]:
        def share(m, j, code):
            spot = outs[m].at[toggled_all(me_roll, code)]
            return pltpu.make_async_remote_copy(
                src_ref=spot, dst_ref=spot,
                send_sem=share_send.at[m, index + j], recv_sem=share_recv.at[m, index + j],
                device_id=peer(direction), device_id_type=pl.DeviceIdType.MESH,
            )

        for m in range(mats):
            for j, code in enumerate(held):
                share(m, j, code).start()
        for m in range(mats):
            for j, code in enumerate(held):
                share(m, j, code).wait()
        index += len(held)
        held = held + [code ^ direction[1] for code in held]


def toggled_all(value, code):
    return toggled(value, code, 1) if code else value


def reduce_all(parts, n_tm, n_roll, call_id):
    blocks = n_tm * n_roll
    kept = blocks // 2
    count = kept.bit_length() - 1
    shapes = [(p.shape[0] // blocks, p.shape[1]) for p in parts]
    half = jnp.bfloat16
    cubes = [p.reshape((blocks,) + s) for p, s in zip(parts, shapes)]
    sem = pltpu.SemaphoreType.DMA
    outs = pl.pallas_call(
        functools.partial(reduce_kernel, n_tm, n_roll),
        out_shape=[jax.ShapeDtypeStruct((n_roll,) + s, half) for s in shapes],
        in_specs=[pl.BlockSpec(memory_space=pl.ANY)] * 4,
        out_specs=[pl.BlockSpec(memory_space=pltpu.VMEM)] * 4,
        scratch_shapes=[pltpu.VMEM((kept,) + s, half) for s in shapes] * 3
        + [
            sem((4,)), sem((4,)), sem((4,)), sem((4, count)), sem((4, count)),
            sem((4, n_roll)), sem((4, n_roll)),
        ],
        compiler_params=pltpu.CompilerParams(
            collective_id=call_id, has_side_effects=True, vmem_limit_bytes=40 * 2**20
        ),
        cost_estimate=pl.CostEstimate(
            flops=0, bytes_accessed=40 * sum(2 * p.size for p in parts), transcendentals=0
        ),
        name="reduce_all",
    )(*cubes)
    return [o.reshape(o.shape[0] * o.shape[1], o.shape[2]) for o in outs]


def partial_kernel(x_ref, g_ref, low_ref, high_ref):
    total = dot_first(x_ref[...], g_ref[...]).astype(jnp.bfloat16)
    half = total.shape[1] // 2
    low_ref[...] = total[:, :half]
    high_ref[...] = total[:, half:]


def partial_halves(left, right):
    rows, depth = left.shape
    width = right.shape[1]
    tile = min(256, depth)
    half = jax.ShapeDtypeStruct((depth, width // 2), jnp.bfloat16)
    return pl.pallas_call(
        partial_kernel,
        grid=(depth // tile,),
        in_specs=[
            pl.BlockSpec((rows, tile), lambda i: (0, i)),
            pl.BlockSpec((rows, width), lambda i: (0, 0)),
        ],
        out_specs=[pl.BlockSpec((tile, width // 2), lambda i: (i, 0))] * 2,
        out_shape=[half, half],
        compiler_params=pltpu.CompilerParams(vmem_limit_bytes=24 * 2**20),
        cost_estimate=pl.CostEstimate(
            flops=2 * rows * depth * width,
            bytes_accessed=2 * (depth * width + rows * depth + rows * width),
            transcendentals=0,
        ),
        name="partial_halves",
    )(left, right)


def lists_kernel(n_tm, lists_ref, all_ref, local_sem, send_sem, recv_sem):
    me = lax.axis_index("tm")
    barrier = pltpu.get_barrier_semaphore()
    for d in range(1, n_tm):
        pl.semaphore_signal(
            barrier, inc=1, device_id={"tm": (me + d) % n_tm},
            device_id_type=pl.DeviceIdType.MESH,
        )
    mine = pltpu.make_async_copy(lists_ref, all_ref.at[me], local_sem)
    mine.start()
    pl.semaphore_wait(barrier, n_tm - 1)
    copies = [
        pltpu.make_async_remote_copy(
            src_ref=lists_ref, dst_ref=all_ref.at[me],
            send_sem=send_sem.at[d], recv_sem=recv_sem.at[d],
            device_id={"tm": (me + d) % n_tm}, device_id_type=pl.DeviceIdType.MESH,
        )
        for d in range(1, n_tm)
    ]
    for copy in copies:
        copy.start()
    mine.wait()
    for copy in copies:
        copy.wait()


def gather_lists(lists, n_tm):
    return pl.pallas_call(
        functools.partial(lists_kernel, n_tm),
        out_shape=jax.ShapeDtypeStruct((n_tm,) + lists.shape, lists.dtype),
        in_specs=[pl.BlockSpec(memory_space=pltpu.VMEM)],
        out_specs=pl.BlockSpec(memory_space=pltpu.VMEM),
        scratch_shapes=[
            pltpu.SemaphoreType.DMA,
            pltpu.SemaphoreType.DMA((n_tm,)),
            pltpu.SemaphoreType.DMA((n_tm,)),
        ],
        compiler_params=pltpu.CompilerParams(collective_id=2, has_side_effects=True),
        name="gather_lists",
    )(lists)


def local(inputs, cotangent, memory_lists, w_query, w_key, w_value, w_output):
    frame_count, frame_tokens, model_width = inputs.shape[1:]
    inner_width = w_query.shape[1]
    blocks = lax.axis_size("tm")
    position = lax.axis_index("tm")
    row_count = frame_count * frame_tokens
    flat_input = inputs.reshape(row_count, model_width)
    grad_flat = cotangent.reshape(row_count, model_width)
    queries = jnp.dot(flat_input, w_query, preferred_element_type=jnp.float32).astype(jnp.bfloat16)
    key_rows = jnp.dot(flat_input, w_key, preferred_element_type=jnp.float32).astype(jnp.bfloat16)
    value_rows = jnp.dot(flat_input, w_value, preferred_element_type=jnp.float32).astype(
        jnp.bfloat16
    )
    grad_heads = dot_last(grad_flat, w_output).astype(jnp.bfloat16)
    recalled = memory_lists[0]
    first_frame = position * frame_count
    last_rows = BAND * frame_tokens
    last_frames = jnp.concatenate(
        [key_rows[row_count - last_rows :], value_rows[row_count - last_rows :]], axis=-1
    )
    before = from_behind(last_frames, "tm", 1)
    all_lists = gather_lists(recalled, blocks)
    targets = jnp.arange(blocks * frame_count, dtype=jnp.int32)
    wanted = jnp.any(recalled.reshape(-1, 1) == targets[None, :], axis=0).reshape(
        blocks, frame_count
    )
    slot_rank = jnp.cumsum(wanted.astype(jnp.int32), axis=1) - 1
    mem_ok = recalled >= 0
    slot_frame = jnp.where(
        wanted[:, None, :] & (slot_rank[:, None, :] == jnp.arange(CAP, dtype=jnp.int32)[:, None]),
        targets.reshape(blocks, 1, frame_count) + 1,
        0,
    ).sum(axis=-1).reshape(-1) - 1
    slot_ok = jnp.any(
        mem_ok[:, :, None] & (recalled[:, :, None] == slot_frame[None, None, :]), axis=1
    )
    pool_frame = first_frame + jnp.concatenate(
        [jnp.arange(frame_count, dtype=jnp.int32), jnp.arange(-BAND, 0, dtype=jnp.int32)]
    )
    ahead = (first_frame + jnp.arange(frame_count, dtype=jnp.int32))[:, None] - pool_frame[None, :]
    band_ok = (ahead >= 0) & (ahead <= BAND) & (pool_frame >= 0)[None, :]
    frame_ok = jnp.concatenate([band_ok, slot_ok], axis=1)
    bias = jnp.where(frame_ok, 0.0, masked_score).astype(jnp.float32)
    bias = jnp.repeat(jnp.repeat(bias, frame_tokens, axis=0), frame_tokens, axis=1)
    own_frames = first_frame + jnp.arange(frame_count, dtype=jnp.int32)
    requested = jnp.any(
        all_lists.reshape(blocks, frame_count * MEM, 1) == own_frames[None, None, :], axis=1
    )
    asked_rank = jnp.cumsum(requested.astype(jnp.int32), axis=1) - 1
    picker = requested[:, None, :] & (
        asked_rank[:, None, :] == jnp.arange(CAP, dtype=jnp.int32)[None, :, None]
    )
    picker = picker.astype(jnp.bfloat16)
    out_keys = jnp.einsum(
        "bcp,pz->bcz", picker, key_rows.reshape(frame_count, -1), preferred_element_type=jnp.float32
    )
    out_values = jnp.einsum(
        "bcp,pz->bcz",
        picker,
        value_rows.reshape(frame_count, -1),
        preferred_element_type=jnp.float32,
    )
    piece_shape = (blocks, CAP, frame_tokens, inner_width)
    outgoing = jnp.concatenate(
        [
            out_keys.astype(jnp.bfloat16).reshape(piece_shape),
            out_values.astype(jnp.bfloat16).reshape(piece_shape),
        ],
        axis=-1,
    )
    incoming = lax.all_to_all(outgoing, "tm", split_axis=0, concat_axis=0, tiled=True)
    slot_rows = incoming.reshape(blocks * CAP * frame_tokens, 2 * inner_width)
    (
        heads_rows, query_rows, own_keys, own_values, rim_keys, rim_values, slot_keys, slot_values
    ) = attend(queries, grad_heads, key_rows, value_rows, before, slot_rows, bias)
    rim = jnp.concatenate([rim_keys, rim_values], axis=-1)
    passed = from_behind(rim, "tm", -1)
    slot_grad = jnp.concatenate([slot_keys, slot_values], axis=-1).reshape(piece_shape[:3] + (-1,))
    returned = lax.all_to_all(slot_grad, "tm", split_axis=0, concat_axis=0, tiled=True)
    rollouts = lax.axis_size("roll")
    early = reduce_all(
        partial_halves(flat_input, query_rows) + partial_halves(heads_rows, grad_flat),
        blocks, rollouts, 0,
    )
    returned, passed, early = lax.optimization_barrier((returned, passed, early))
    passed_full = jnp.pad(passed.astype(jnp.float32), ((row_count - last_rows, 0), (0, 0)))
    gathered_back = jnp.einsum(
        "bcp,bcz->pz", picker, returned.reshape(blocks, CAP, -1), preferred_element_type=jnp.float32
    )
    gathered_back = gathered_back.reshape(row_count, 2 * inner_width)
    grad_keys = (
        own_keys + passed_full[..., :inner_width] + gathered_back[..., :inner_width]
    ).astype(jnp.bfloat16)
    grad_values = (
        own_values + passed_full[..., inner_width:] + gathered_back[..., inner_width:]
    ).astype(jnp.bfloat16)
    grad_input = (
        dot_last(query_rows, w_query) + dot_last(grad_keys, w_key) + dot_last(grad_values, w_value)
    )
    grad_input = grad_input.astype(jnp.bfloat16).reshape(1, frame_count, frame_tokens, model_width)
    attended = jnp.dot(heads_rows, w_output, preferred_element_type=jnp.float32).astype(
        jnp.bfloat16
    )
    attended = attended.reshape(1, frame_count, frame_tokens, model_width)
    late = reduce_all(
        partial_halves(flat_input, grad_keys) + partial_halves(flat_input, grad_values),
        blocks, rollouts, 1,
    )
    totals = [
        jnp.concatenate(pieces, axis=1).astype(jnp.float32)
        for pieces in (early[:2], late[:2], late[2:], early[2:])
    ]
    return (attended, grad_input, totals[0], totals[1], totals[2], totals[3])


def solution(mesh):
    return jax.shard_map(
        local,
        mesh=mesh,
        in_specs=(
            P("roll", "tm", None, None),
            P("roll", "tm", None, None),
            P("roll", "tm", None),
            P(),
            P(),
            P(),
            P(),
        ),
        out_specs=(
            P("roll", "tm", None, None),
            P("roll", "tm", None, None),
            P("tm", None),
            P("tm", None),
            P("tm", None),
            P("tm", None),
        ),
        check_vma=False,
    )
```

```python
import functools

import jax
import jax.numpy as jnp
from jax import lax
from jax.experimental import pallas as pl
from jax.experimental.pallas import tpu as pltpu
from jax.sharding import PartitionSpec as P

HEADS = 8
HEAD = 128
BAND = 4
MEM = 8
CAP = 3


masked_score = -1e30


def from_behind(block, axis, distance):
    devices = range(lax.axis_size(axis))
    route = [(i - distance, i) for i in devices if i - distance in devices]
    return lax.ppermute(block, axis, route)


def dot_last(left, right):
    return lax.dot_general(
        left, right, (((1,), (1,)), ((), ())), preferred_element_type=jnp.float32
    )


def dot_first(left, right):
    return lax.dot_general(
        left, right, (((0,), (0,)), ((), ())), preferred_element_type=jnp.float32
    )


def attend_kernel(q_ref, g_ref, ko_ref, vo_ref, kb_ref, vb_ref, ks_ref, vs_ref, bias_ref,
                  out_ref, gq_ref, gko_ref, gvo_ref, gkb_ref, gvb_ref, gks_ref, gvs_ref):
    scale = HEAD ** (-0.5)
    q = q_ref[...]
    g = g_ref[...]
    k = jnp.concatenate([ko_ref[...], kb_ref[...], ks_ref[...]], axis=0)
    v = jnp.concatenate([vo_ref[...], vb_ref[...], vs_ref[...]], axis=0)
    scores = dot_last(q, k) * scale + bias_ref[...]
    weights = jnp.exp(scores - jnp.max(scores, axis=-1, keepdims=True))
    weights = weights * (1.0 / jnp.sum(weights, axis=-1, keepdims=True))
    rounded = weights.astype(jnp.bfloat16)
    out_ref[...] = jnp.dot(rounded, v, preferred_element_type=jnp.float32).astype(jnp.bfloat16)
    grad_prob = dot_last(g, v)
    row_dot = jnp.sum(weights * grad_prob, axis=-1, keepdims=True)
    dscore = (weights * (grad_prob - row_dot)).astype(jnp.bfloat16)
    gq = jnp.dot(dscore, k, preferred_element_type=jnp.float32) * scale
    gq_ref[...] = gq.astype(jnp.bfloat16)
    gk = dot_first(dscore, q) * scale
    gv = dot_first(rounded, g)
    own = ko_ref.shape[0]
    ext = own + kb_ref.shape[0]
    gko_ref[...] = gk[:own]
    gvo_ref[...] = gv[:own]
    gkb_ref[...] = gk[own:ext].astype(jnp.bfloat16)
    gvb_ref[...] = gv[own:ext].astype(jnp.bfloat16)
    gks_ref[...] = gk[ext:].astype(jnp.bfloat16)
    gvs_ref[...] = gv[ext:].astype(jnp.bfloat16)


def attend(queries, grad_heads, key_own, value_own, before, slots, bias):
    rows, width = queries.shape
    heads = width // HEAD

    def column(count, shift=0):
        return pl.BlockSpec((count, HEAD), lambda h: (0, h + shift))

    nb, ns = before.shape[0], slots.shape[0]
    pool = rows + nb + ns
    half = jnp.bfloat16
    return pl.pallas_call(
        attend_kernel,
        grid=(heads,),
        in_specs=[
            column(rows), column(rows), column(rows), column(rows),
            column(nb), column(nb, heads), column(ns), column(ns, heads),
            pl.BlockSpec((rows, pool), lambda h: (0, 0)),
        ],
        out_specs=[
            column(rows), column(rows), column(rows), column(rows),
            column(nb), column(nb), column(ns), column(ns),
        ],
        out_shape=[
            jax.ShapeDtypeStruct((rows, width), half),
            jax.ShapeDtypeStruct((rows, width), half),
            jax.ShapeDtypeStruct((rows, width), jnp.float32),
            jax.ShapeDtypeStruct((rows, width), jnp.float32),
            jax.ShapeDtypeStruct((nb, width), half),
            jax.ShapeDtypeStruct((nb, width), half),
            jax.ShapeDtypeStruct((ns, width), half),
            jax.ShapeDtypeStruct((ns, width), half),
        ],
        compiler_params=pltpu.CompilerParams(vmem_limit_bytes=56 * 2**20),
        cost_estimate=pl.CostEstimate(
            flops=12 * rows * pool * width,
            bytes_accessed=8 * pool * width,
            transcendentals=heads * rows * pool,
        ),
        name="attend",
    )(queries, grad_heads, key_own, value_own, before, before, slots, slots, bias)


def toggled(value, mask, bit):
    k = 0
    while (1 << k) <= mask:
        if (mask >> k) & 1:
            step = 1 << k
            value = value + bit * step * (1 - 2 * ((value // step) % 2))
        k += 1
    return value


def masks_of(size):
    masks = []
    k = 0
    while (1 << k) < size:
        masks.append((1 << k) if k < 2 else (1 << k) + (1 << (k - 1)))
        k += 1
    return masks


def reduce_kernel(n_tm, n_roll, across_first, *refs):
    mats = 4
    parts, refs = refs[:mats], refs[mats:]
    outs, refs = refs[:mats], refs[mats:]
    own, refs = refs[:mats], refs[mats:]
    far, refs = refs[:mats], refs[mats:]
    local_sem, far_send, far_recv, share_send, share_recv = refs

    me_tm = lax.axis_index("tm")
    me_roll = lax.axis_index("roll")
    pair = ("roll", 1)
    roll_rest = [("roll", m) for m in masks_of(n_roll)[1:]]
    others = roll_rest + [("tm", m) for m in masks_of(n_tm)]
    count = len(others)
    kept = 1 << count

    def peer(direction):
        axis, mask = direction
        mine = me_tm if axis == "tm" else me_roll
        return {axis: toggled(mine, mask, 1)}

    barrier = pltpu.get_barrier_semaphore()
    for direction in [pair] + others:
        pl.semaphore_signal(
            barrier, inc=1, device_id=peer(direction), device_id_type=pl.DeviceIdType.MESH
        )
    pl.semaphore_wait(barrier, 1 + count)

    def order(m):
        if across_first:
            return others if m % 2 == 0 else others[1::-1] + others[:1:-1]
        shift = m % count
        return others[shift:] + others[:shift]

    def block_of(m, position):
        tm, roll = me_tm, me_roll
        for i, (axis, mask) in enumerate(order(m)):
            bit = (position // (1 << (count - 1 - i))) % 2
            if axis == "tm":
                tm = toggled(tm, mask, bit)
            else:
                roll = toggled(roll, mask, bit)
        return tm * (n_roll // 2) + roll // 2

    def far_copy(m, s):
        size = kept >> (s + 1)
        return pltpu.make_async_remote_copy(
            src_ref=own[m].at[pl.ds(size, size)],
            dst_ref=far[m].at[pl.ds(size, size)],
            send_sem=far_send.at[m, s], recv_sem=far_recv.at[m, s],
            device_id=peer(order(m)[s]), device_id_type=pl.DeviceIdType.MESH,
        )

    for m in range(mats):
        @pl.loop(0, kept)
        def _(position):
            pltpu.make_async_copy(
                parts[m].at[block_of(m, position)], own[m].at[position], local_sem.at[m]
            ).start()

    def add(target, source, length, offset):
        @pl.loop(0, length)
        def _(i):
            total = target[i].astype(jnp.float32) + source[i + offset].astype(jnp.float32)
            target[i] = total.astype(jnp.bfloat16)

    for m in range(mats):
        pltpu.make_async_copy(parts[m], own[m], local_sem.at[m]).wait()
        far_copy(m, 0).start()

    for s in range(count):
        for m in range(mats):
            far_copy(m, s).wait()
            size = kept >> (s + 1)
            add(own[m], far[m], size, size)
            if s + 1 < count:
                far_copy(m, s + 1).start()

    for m in range(mats):
        outs[m][me_roll] = own[m][0]
    held = [0]
    index = 0
    for direction in roll_rest[::-1] + [pair]:
        def share(m, j, code):
            spot = outs[m].at[toggled_all(me_roll, code)]
            return pltpu.make_async_remote_copy(
                src_ref=spot, dst_ref=spot,
                send_sem=share_send.at[m, index + j], recv_sem=share_recv.at[m, index + j],
                device_id=peer(direction), device_id_type=pl.DeviceIdType.MESH,
            )

        for m in range(mats):
            for j, code in enumerate(held):
                share(m, j, code).start()
        for m in range(mats):
            for j, code in enumerate(held):
                share(m, j, code).wait()
        index += len(held)
        held = held + [code ^ direction[1] for code in held]


def toggled_all(value, code):
    return toggled(value, code, 1) if code else value


def reduce_all(parts, n_tm, n_roll, call_id):
    kept = n_tm * n_roll // 2
    blocks = kept
    count = kept.bit_length() - 1
    shapes = [(p.shape[0] // blocks, p.shape[1]) for p in parts]
    half = jnp.bfloat16
    cubes = [p.reshape((blocks,) + s) for p, s in zip(parts, shapes)]
    sem = pltpu.SemaphoreType.DMA
    outs = pl.pallas_call(
        functools.partial(reduce_kernel, n_tm, n_roll, call_id == 0),
        out_shape=[jax.ShapeDtypeStruct((n_roll,) + s, half) for s in shapes],
        in_specs=[pl.BlockSpec(memory_space=pl.ANY)] * 4,
        out_specs=[pl.BlockSpec(memory_space=pltpu.VMEM)] * 4,
        scratch_shapes=[pltpu.VMEM((kept,) + s, half) for s in shapes] * 2
        + [
            sem((4,)), sem((4, count)), sem((4, count)),
            sem((4, n_roll)), sem((4, n_roll)),
        ],
        compiler_params=pltpu.CompilerParams(
            collective_id=call_id, has_side_effects=True, vmem_limit_bytes=40 * 2**20
        ),
        cost_estimate=pl.CostEstimate(
            flops=0, bytes_accessed=40 * sum(2 * p.size for p in parts), transcendentals=0
        ),
        name="reduce_all",
    )(*cubes)
    return outs


def assembled(low, high):
    n_roll, rows, width = low.shape
    both = jnp.stack([low, high], axis=2).reshape(n_roll // 2, 2, rows, 2 * width)
    return both.transpose(0, 2, 1, 3).reshape(n_roll // 2 * rows, 4 * width).astype(jnp.float32)


def from_pair(block):
    return lax.ppermute(block, "roll", [(i, i ^ 1) for i in range(lax.axis_size("roll"))])


def column_halves(block):
    half = block.shape[1] // 2
    core = lax.axis_index("roll") % 2
    return (
        lax.dynamic_slice_in_dim(block, core * half, half, 1),
        lax.dynamic_slice_in_dim(block, (1 - core) * half, half, 1),
    )


def partial_kernel(x_ref, y_ref, g_ref, h_ref, low_ref, high_ref):
    total = dot_first(x_ref[...], g_ref[...]) + dot_first(y_ref[...], h_ref[...])
    total = total.astype(jnp.bfloat16)
    half = total.shape[1] // 2
    low_ref[...] = total[:, :half]
    high_ref[...] = total[:, half:]


def partial_halves(left, left_pair, right, right_pair):
    rows, depth = left.shape
    width = right.shape[1]
    tile = min(256, depth)
    half = jax.ShapeDtypeStruct((depth, width // 2), jnp.bfloat16)
    left_spec = pl.BlockSpec((rows, tile), lambda i: (0, i))
    right_spec = pl.BlockSpec((rows, width), lambda i: (0, 0))
    return pl.pallas_call(
        partial_kernel,
        grid=(depth // tile,),
        in_specs=[left_spec, left_spec, right_spec, right_spec],
        out_specs=[pl.BlockSpec((tile, width // 2), lambda i: (i, 0))] * 2,
        out_shape=[half, half],
        compiler_params=pltpu.CompilerParams(vmem_limit_bytes=24 * 2**20),
        cost_estimate=pl.CostEstimate(
            flops=4 * rows * depth * width,
            bytes_accessed=2 * (depth * width + 2 * rows * depth + 2 * rows * width),
            transcendentals=0,
        ),
        name="partial_halves",
    )(left, left_pair, right, right_pair)


def lists_kernel(n_tm, lists_ref, all_ref, local_sem, send_sem, recv_sem):
    me = lax.axis_index("tm")
    barrier = pltpu.get_barrier_semaphore()
    for d in range(1, n_tm):
        pl.semaphore_signal(
            barrier, inc=1, device_id={"tm": (me + d) % n_tm},
            device_id_type=pl.DeviceIdType.MESH,
        )
    mine = pltpu.make_async_copy(lists_ref, all_ref.at[me], local_sem)
    mine.start()
    pl.semaphore_wait(barrier, n_tm - 1)
    copies = [
        pltpu.make_async_remote_copy(
            src_ref=lists_ref, dst_ref=all_ref.at[me],
            send_sem=send_sem.at[d], recv_sem=recv_sem.at[d],
            device_id={"tm": (me + d) % n_tm}, device_id_type=pl.DeviceIdType.MESH,
        )
        for d in range(1, n_tm)
    ]
    for copy in copies:
        copy.start()
    mine.wait()
    for copy in copies:
        copy.wait()


def gather_lists(lists, n_tm):
    return pl.pallas_call(
        functools.partial(lists_kernel, n_tm),
        out_shape=jax.ShapeDtypeStruct((n_tm,) + lists.shape, lists.dtype),
        in_specs=[pl.BlockSpec(memory_space=pltpu.VMEM)],
        out_specs=pl.BlockSpec(memory_space=pltpu.VMEM),
        scratch_shapes=[
            pltpu.SemaphoreType.DMA,
            pltpu.SemaphoreType.DMA((n_tm,)),
            pltpu.SemaphoreType.DMA((n_tm,)),
        ],
        compiler_params=pltpu.CompilerParams(collective_id=2, has_side_effects=True),
        name="gather_lists",
    )(lists)


def local(inputs, cotangent, memory_lists, w_query, w_key, w_value, w_output):
    frame_count, frame_tokens, model_width = inputs.shape[1:]
    inner_width = w_query.shape[1]
    blocks = lax.axis_size("tm")
    position = lax.axis_index("tm")
    row_count = frame_count * frame_tokens
    flat_input = inputs.reshape(row_count, model_width)
    grad_flat = cotangent.reshape(row_count, model_width)
    queries = jnp.dot(flat_input, w_query, preferred_element_type=jnp.float32).astype(jnp.bfloat16)
    key_rows = jnp.dot(flat_input, w_key, preferred_element_type=jnp.float32).astype(jnp.bfloat16)
    value_rows = jnp.dot(flat_input, w_value, preferred_element_type=jnp.float32).astype(
        jnp.bfloat16
    )
    grad_heads = dot_last(grad_flat, w_output).astype(jnp.bfloat16)
    input_pair = from_pair(flat_input)
    grad_keep, grad_give = column_halves(grad_flat)
    grad_pair = from_pair(grad_give)
    recalled = memory_lists[0]
    first_frame = position * frame_count
    last_rows = BAND * frame_tokens
    last_frames = jnp.concatenate(
        [key_rows[row_count - last_rows :], value_rows[row_count - last_rows :]], axis=-1
    )
    before = from_behind(last_frames, "tm", 1)
    all_lists = gather_lists(recalled, blocks)
    targets = jnp.arange(blocks * frame_count, dtype=jnp.int32)
    wanted = jnp.any(recalled.reshape(-1, 1) == targets[None, :], axis=0).reshape(
        blocks, frame_count
    )
    slot_rank = jnp.cumsum(wanted.astype(jnp.int32), axis=1) - 1
    mem_ok = recalled >= 0
    slot_frame = jnp.where(
        wanted[:, None, :] & (slot_rank[:, None, :] == jnp.arange(CAP, dtype=jnp.int32)[:, None]),
        targets.reshape(blocks, 1, frame_count) + 1,
        0,
    ).sum(axis=-1).reshape(-1) - 1
    slot_ok = jnp.any(
        mem_ok[:, :, None] & (recalled[:, :, None] == slot_frame[None, None, :]), axis=1
    )
    pool_frame = first_frame + jnp.concatenate(
        [jnp.arange(frame_count, dtype=jnp.int32), jnp.arange(-BAND, 0, dtype=jnp.int32)]
    )
    ahead = (first_frame + jnp.arange(frame_count, dtype=jnp.int32))[:, None] - pool_frame[None, :]
    band_ok = (ahead >= 0) & (ahead <= BAND) & (pool_frame >= 0)[None, :]
    frame_ok = jnp.concatenate([band_ok, slot_ok], axis=1)
    bias = jnp.where(frame_ok, 0.0, masked_score).astype(jnp.float32)
    bias = jnp.repeat(jnp.repeat(bias, frame_tokens, axis=0), frame_tokens, axis=1)
    own_frames = first_frame + jnp.arange(frame_count, dtype=jnp.int32)
    requested = jnp.any(
        all_lists.reshape(blocks, frame_count * MEM, 1) == own_frames[None, None, :], axis=1
    )
    asked_rank = jnp.cumsum(requested.astype(jnp.int32), axis=1) - 1
    picker = requested[:, None, :] & (
        asked_rank[:, None, :] == jnp.arange(CAP, dtype=jnp.int32)[None, :, None]
    )
    picker = picker.astype(jnp.bfloat16)
    out_keys = jnp.einsum(
        "bcp,pz->bcz", picker, key_rows.reshape(frame_count, -1), preferred_element_type=jnp.float32
    )
    out_values = jnp.einsum(
        "bcp,pz->bcz",
        picker,
        value_rows.reshape(frame_count, -1),
        preferred_element_type=jnp.float32,
    )
    piece_shape = (blocks, CAP, frame_tokens, inner_width)
    outgoing = jnp.concatenate(
        [
            out_keys.astype(jnp.bfloat16).reshape(piece_shape),
            out_values.astype(jnp.bfloat16).reshape(piece_shape),
        ],
        axis=-1,
    )
    incoming = lax.all_to_all(outgoing, "tm", split_axis=0, concat_axis=0, tiled=True)
    incoming, before, input_pair, grad_pair = lax.optimization_barrier(
        (incoming, before, input_pair, grad_pair)
    )
    slot_rows = incoming.reshape(blocks * CAP * frame_tokens, 2 * inner_width)
    (
        heads_rows, query_rows, own_keys, own_values, rim_keys, rim_values, slot_keys, slot_values
    ) = attend(queries, grad_heads, key_rows, value_rows, before, slot_rows, bias)
    rim = jnp.concatenate([rim_keys, rim_values], axis=-1)
    passed = from_behind(rim, "tm", -1)
    slot_grad = jnp.concatenate([slot_keys, slot_values], axis=-1).reshape(piece_shape[:3] + (-1,))
    returned = lax.all_to_all(slot_grad, "tm", split_axis=0, concat_axis=0, tiled=True)
    rollouts = lax.axis_size("roll")
    query_keep, query_give = column_halves(query_rows)
    early = reduce_all(
        partial_halves(flat_input, input_pair, query_keep, from_pair(query_give))
        + partial_halves(heads_rows, from_pair(heads_rows), grad_keep, grad_pair),
        blocks, rollouts, 0,
    )
    returned, passed, early = lax.optimization_barrier((returned, passed, early))
    passed_full = jnp.pad(passed.astype(jnp.float32), ((row_count - last_rows, 0), (0, 0)))
    gathered_back = jnp.einsum(
        "bcp,bcz->pz", picker, returned.reshape(blocks, CAP, -1), preferred_element_type=jnp.float32
    )
    gathered_back = gathered_back.reshape(row_count, 2 * inner_width)
    grad_keys = (
        own_keys + passed_full[..., :inner_width] + gathered_back[..., :inner_width]
    ).astype(jnp.bfloat16)
    grad_values = (
        own_values + passed_full[..., inner_width:] + gathered_back[..., inner_width:]
    ).astype(jnp.bfloat16)
    grad_input = (
        dot_last(query_rows, w_query) + dot_last(grad_keys, w_key) + dot_last(grad_values, w_value)
    )
    grad_input = grad_input.astype(jnp.bfloat16).reshape(1, frame_count, frame_tokens, model_width)
    attended = jnp.dot(heads_rows, w_output, preferred_element_type=jnp.float32).astype(
        jnp.bfloat16
    )
    attended = attended.reshape(1, frame_count, frame_tokens, model_width)
    key_keep, key_give = column_halves(grad_keys)
    value_keep, value_give = column_halves(grad_values)
    late = reduce_all(
        partial_halves(flat_input, input_pair, key_keep, from_pair(key_give))
        + partial_halves(flat_input, input_pair, value_keep, from_pair(value_give)),
        blocks, rollouts, 1,
    )
    totals = [
        assembled(*pieces)
        for pieces in (early[:2], late[:2], late[2:], early[2:])
    ]
    return (attended, grad_input, totals[0], totals[1], totals[2], totals[3])


def solution(mesh):
    return jax.shard_map(
        local,
        mesh=mesh,
        in_specs=(
            P("roll", "tm", None, None),
            P("roll", "tm", None, None),
            P("roll", "tm", None),
            P(),
            P(),
            P(),
            P(),
        ),
        out_specs=(
            P("roll", "tm", None, None),
            P("roll", "tm", None, None),
            P("tm", None),
            P("tm", None),
            P("tm", None),
            P("tm", None),
        ),
        check_vma=False,
    )
```

```python
import functools

import jax
import jax.numpy as jnp
from jax import lax
from jax.experimental import pallas as pl
from jax.experimental.pallas import tpu as pltpu
from jax.sharding import PartitionSpec as P

HEADS = 8
HEAD = 128
BAND = 4
MEM = 8
CAP = 3


masked_score = -1e30


def from_behind(block, axis, distance):
    devices = range(lax.axis_size(axis))
    route = [(i - distance, i) for i in devices if i - distance in devices]
    return lax.ppermute(block, axis, route)


def dot_last(left, right):
    return lax.dot_general(
        left, right, (((1,), (1,)), ((), ())), preferred_element_type=jnp.float32
    )


def dot_first(left, right):
    return lax.dot_general(
        left, right, (((0,), (0,)), ((), ())), preferred_element_type=jnp.float32
    )


def attend_kernel(q_ref, g_ref, ko_ref, vo_ref, kb_ref, vb_ref, ks_ref, vs_ref, bias_ref,
                  out_ref, gq_ref, gko_ref, gvo_ref, gkb_ref, gvb_ref, gks_ref, gvs_ref):
    scale = HEAD ** (-0.5)
    q = q_ref[...]
    g = g_ref[...]
    k = jnp.concatenate([ko_ref[...], kb_ref[...], ks_ref[...]], axis=0)
    v = jnp.concatenate([vo_ref[...], vb_ref[...], vs_ref[...]], axis=0)
    scores = dot_last(q, k) * scale + bias_ref[...]
    weights = jnp.exp(scores - jnp.max(scores, axis=-1, keepdims=True))
    weights = weights * (1.0 / jnp.sum(weights, axis=-1, keepdims=True))
    rounded = weights.astype(jnp.bfloat16)
    out_ref[...] = jnp.dot(rounded, v, preferred_element_type=jnp.float32).astype(jnp.bfloat16)
    grad_prob = dot_last(g, v)
    row_dot = jnp.sum(weights * grad_prob, axis=-1, keepdims=True)
    dscore = (weights * (grad_prob - row_dot)).astype(jnp.bfloat16)
    gq = jnp.dot(dscore, k, preferred_element_type=jnp.float32) * scale
    gq_ref[...] = gq.astype(jnp.bfloat16)
    gk = dot_first(dscore, q) * scale
    gv = dot_first(rounded, g)
    own = ko_ref.shape[0]
    ext = own + kb_ref.shape[0]
    gko_ref[...] = gk[:own]
    gvo_ref[...] = gv[:own]
    gkb_ref[...] = gk[own:ext].astype(jnp.bfloat16)
    gvb_ref[...] = gv[own:ext].astype(jnp.bfloat16)
    gks_ref[...] = gk[ext:].astype(jnp.bfloat16)
    gvs_ref[...] = gv[ext:].astype(jnp.bfloat16)


def attend(queries, grad_heads, key_own, value_own, before, slots, bias):
    rows, width = queries.shape
    heads = width // HEAD

    def column(count, shift=0):
        return pl.BlockSpec((count, HEAD), lambda h: (0, h + shift))

    nb, ns = before.shape[0], slots.shape[0]
    pool = rows + nb + ns
    half = jnp.bfloat16
    return pl.pallas_call(
        attend_kernel,
        grid=(heads,),
        in_specs=[
            column(rows), column(rows), column(rows), column(rows),
            column(nb), column(nb, heads), column(ns), column(ns, heads),
            pl.BlockSpec((rows, pool), lambda h: (0, 0)),
        ],
        out_specs=[
            column(rows), column(rows), column(rows), column(rows),
            column(nb), column(nb), column(ns), column(ns),
        ],
        out_shape=[
            jax.ShapeDtypeStruct((rows, width), half),
            jax.ShapeDtypeStruct((rows, width), half),
            jax.ShapeDtypeStruct((rows, width), jnp.float32),
            jax.ShapeDtypeStruct((rows, width), jnp.float32),
            jax.ShapeDtypeStruct((nb, width), half),
            jax.ShapeDtypeStruct((nb, width), half),
            jax.ShapeDtypeStruct((ns, width), half),
            jax.ShapeDtypeStruct((ns, width), half),
        ],
        compiler_params=pltpu.CompilerParams(vmem_limit_bytes=56 * 2**20),
        cost_estimate=pl.CostEstimate(
            flops=12 * rows * pool * width,
            bytes_accessed=8 * pool * width,
            transcendentals=heads * rows * pool,
        ),
        name="attend",
    )(queries, grad_heads, key_own, value_own, before, before, slots, slots, bias)


def toggled(value, mask, bit):
    k = 0
    while (1 << k) <= mask:
        if (mask >> k) & 1:
            step = 1 << k
            value = value + bit * step * (1 - 2 * ((value // step) % 2))
        k += 1
    return value


def masks_of(size):
    masks = []
    k = 0
    while (1 << k) < size:
        masks.append((1 << k) if k < 2 else (1 << k) + (1 << (k - 1)))
        k += 1
    return masks


def reduce_kernel(n_tm, n_roll, across_first, *refs):
    mats = 4
    parts, refs = refs[:mats], refs[mats:]
    outs, refs = refs[:mats], refs[mats:]
    own, refs = refs[:mats], refs[mats:]
    far, refs = refs[:mats], refs[mats:]
    local_sem, far_send, far_recv, share_send, share_recv = refs

    me_tm = lax.axis_index("tm")
    me_roll = lax.axis_index("roll")
    pair = ("roll", 1)
    roll_rest = [("roll", m) for m in masks_of(n_roll)[1:]]
    others = roll_rest + [("tm", m) for m in masks_of(n_tm)]
    count = len(others)
    kept = 1 << count

    def peer(direction):
        axis, mask = direction
        mine = me_tm if axis == "tm" else me_roll
        return {axis: toggled(mine, mask, 1)}

    barrier = pltpu.get_barrier_semaphore()
    for direction in [pair] + others:
        pl.semaphore_signal(
            barrier, inc=1, device_id=peer(direction), device_id_type=pl.DeviceIdType.MESH
        )
    pl.semaphore_wait(barrier, 1 + count)

    def order(m):
        if across_first:
            return others if m % 2 == 0 else others[1::-1] + others[:1:-1]
        shift = m % count
        return others[shift:] + others[:shift]

    def block_of(m, position):
        tm, roll = me_tm, me_roll
        for i, (axis, mask) in enumerate(order(m)):
            bit = (position // (1 << (count - 1 - i))) % 2
            if axis == "tm":
                tm = toggled(tm, mask, bit)
            else:
                roll = toggled(roll, mask, bit)
        return tm * (n_roll // 2) + roll // 2

    def far_copy(m, s):
        size = kept >> (s + 1)
        return pltpu.make_async_remote_copy(
            src_ref=own[m].at[pl.ds(size, size)],
            dst_ref=far[m].at[pl.ds(size, size)],
            send_sem=far_send.at[m, s], recv_sem=far_recv.at[m, s],
            device_id=peer(order(m)[s]), device_id_type=pl.DeviceIdType.MESH,
        )

    for m in range(mats):
        @pl.loop(0, kept)
        def _(position):
            pltpu.make_async_copy(
                parts[m].at[block_of(m, position)], own[m].at[position], local_sem.at[m]
            ).start()

    def add(target, source, length, offset):
        @pl.loop(0, length)
        def _(i):
            total = target[i].astype(jnp.float32) + source[i + offset].astype(jnp.float32)
            target[i] = total.astype(jnp.bfloat16)

    for m in range(mats):
        pltpu.make_async_copy(parts[m], own[m], local_sem.at[m]).wait()
        far_copy(m, 0).start()

    for s in range(count):
        for m in range(mats):
            far_copy(m, s).wait()
            size = kept >> (s + 1)
            add(own[m], far[m], size, size)
            if s + 1 < count:
                far_copy(m, s + 1).start()

    for m in range(mats):
        outs[m][me_roll] = own[m][0]
    held = [0]
    index = 0
    for direction in roll_rest[::-1] + [pair]:
        def share(m, j, code):
            spot = outs[m].at[toggled_all(me_roll, code)]
            return pltpu.make_async_remote_copy(
                src_ref=spot, dst_ref=spot,
                send_sem=share_send.at[m, index + j], recv_sem=share_recv.at[m, index + j],
                device_id=peer(direction), device_id_type=pl.DeviceIdType.MESH,
            )

        for m in range(mats):
            for j, code in enumerate(held):
                share(m, j, code).start()
        for m in range(mats):
            for j, code in enumerate(held):
                share(m, j, code).wait()
        index += len(held)
        held = held + [code ^ direction[1] for code in held]


def toggled_all(value, code):
    return toggled(value, code, 1) if code else value


def reduce_all(parts, n_tm, n_roll, call_id):
    kept = n_tm * n_roll // 2
    blocks = kept
    count = kept.bit_length() - 1
    shapes = [(p.shape[0] // blocks, p.shape[1]) for p in parts]
    half = jnp.bfloat16
    cubes = [p.reshape((blocks,) + s) for p, s in zip(parts, shapes)]
    sem = pltpu.SemaphoreType.DMA
    outs = pl.pallas_call(
        functools.partial(reduce_kernel, n_tm, n_roll, True),
        out_shape=[jax.ShapeDtypeStruct((n_roll,) + s, half) for s in shapes],
        in_specs=[pl.BlockSpec(memory_space=pl.ANY)] * 4,
        out_specs=[pl.BlockSpec(memory_space=pltpu.VMEM)] * 4,
        scratch_shapes=[pltpu.VMEM((kept,) + s, half) for s in shapes] * 2
        + [
            sem((4,)), sem((4, count)), sem((4, count)),
            sem((4, n_roll)), sem((4, n_roll)),
        ],
        compiler_params=pltpu.CompilerParams(
            collective_id=call_id, has_side_effects=True, vmem_limit_bytes=40 * 2**20
        ),
        cost_estimate=pl.CostEstimate(
            flops=0, bytes_accessed=40 * sum(2 * p.size for p in parts), transcendentals=0
        ),
        name="reduce_all",
    )(*cubes)
    return outs


def assembled(low, high):
    n_roll, rows, width = low.shape
    both = jnp.stack([low, high], axis=2).reshape(n_roll // 2, 2, rows, 2 * width)
    return both.transpose(0, 2, 1, 3).reshape(n_roll // 2 * rows, 4 * width).astype(jnp.float32)


def from_pair(block):
    return lax.ppermute(block, "roll", [(i, i ^ 1) for i in range(lax.axis_size("roll"))])


def column_halves(block):
    half = block.shape[1] // 2
    core = lax.axis_index("roll") % 2
    return (
        lax.dynamic_slice_in_dim(block, core * half, half, 1),
        lax.dynamic_slice_in_dim(block, (1 - core) * half, half, 1),
    )


def partial_kernel(x_ref, y_ref, g_ref, h_ref, low_ref, high_ref):
    total = dot_first(x_ref[...], g_ref[...]) + dot_first(y_ref[...], h_ref[...])
    total = total.astype(jnp.bfloat16)
    half = total.shape[1] // 2
    low_ref[...] = total[:, :half]
    high_ref[...] = total[:, half:]


def partial_halves(left, left_pair, right, right_pair):
    rows, depth = left.shape
    width = right.shape[1]
    tile = min(256, depth)
    half = jax.ShapeDtypeStruct((depth, width // 2), jnp.bfloat16)
    left_spec = pl.BlockSpec((rows, tile), lambda i: (0, i))
    right_spec = pl.BlockSpec((rows, width), lambda i: (0, 0))
    return pl.pallas_call(
        partial_kernel,
        grid=(depth // tile,),
        in_specs=[left_spec, left_spec, right_spec, right_spec],
        out_specs=[pl.BlockSpec((tile, width // 2), lambda i: (i, 0))] * 2,
        out_shape=[half, half],
        compiler_params=pltpu.CompilerParams(vmem_limit_bytes=24 * 2**20),
        cost_estimate=pl.CostEstimate(
            flops=4 * rows * depth * width,
            bytes_accessed=2 * (depth * width + 2 * rows * depth + 2 * rows * width),
            transcendentals=0,
        ),
        name="partial_halves",
    )(left, left_pair, right, right_pair)


def lists_kernel(n_tm, lists_ref, all_ref, local_sem, send_sem, recv_sem):
    me = lax.axis_index("tm")
    barrier = pltpu.get_barrier_semaphore()
    for d in range(1, n_tm):
        pl.semaphore_signal(
            barrier, inc=1, device_id={"tm": (me + d) % n_tm},
            device_id_type=pl.DeviceIdType.MESH,
        )
    mine = pltpu.make_async_copy(lists_ref, all_ref.at[me], local_sem)
    mine.start()
    pl.semaphore_wait(barrier, n_tm - 1)
    copies = [
        pltpu.make_async_remote_copy(
            src_ref=lists_ref, dst_ref=all_ref.at[me],
            send_sem=send_sem.at[d], recv_sem=recv_sem.at[d],
            device_id={"tm": (me + d) % n_tm}, device_id_type=pl.DeviceIdType.MESH,
        )
        for d in range(1, n_tm)
    ]
    for copy in copies:
        copy.start()
    mine.wait()
    for copy in copies:
        copy.wait()


def gather_lists(lists, n_tm):
    return pl.pallas_call(
        functools.partial(lists_kernel, n_tm),
        out_shape=jax.ShapeDtypeStruct((n_tm,) + lists.shape, lists.dtype),
        in_specs=[pl.BlockSpec(memory_space=pltpu.VMEM)],
        out_specs=pl.BlockSpec(memory_space=pltpu.VMEM),
        scratch_shapes=[
            pltpu.SemaphoreType.DMA,
            pltpu.SemaphoreType.DMA((n_tm,)),
            pltpu.SemaphoreType.DMA((n_tm,)),
        ],
        compiler_params=pltpu.CompilerParams(collective_id=2, has_side_effects=True),
        name="gather_lists",
    )(lists)


def local(inputs, cotangent, memory_lists, w_query, w_key, w_value, w_output):
    frame_count, frame_tokens, model_width = inputs.shape[1:]
    inner_width = w_query.shape[1]
    blocks = lax.axis_size("tm")
    position = lax.axis_index("tm")
    row_count = frame_count * frame_tokens
    flat_input = inputs.reshape(row_count, model_width)
    grad_flat = cotangent.reshape(row_count, model_width)
    queries = jnp.dot(flat_input, w_query, preferred_element_type=jnp.float32).astype(jnp.bfloat16)
    key_rows = jnp.dot(flat_input, w_key, preferred_element_type=jnp.float32).astype(jnp.bfloat16)
    value_rows = jnp.dot(flat_input, w_value, preferred_element_type=jnp.float32).astype(
        jnp.bfloat16
    )
    grad_heads = dot_last(grad_flat, w_output).astype(jnp.bfloat16)
    input_pair = from_pair(flat_input)
    grad_keep, grad_give = column_halves(grad_flat)
    grad_pair = from_pair(grad_give)
    recalled = memory_lists[0]
    first_frame = position * frame_count
    last_rows = BAND * frame_tokens
    last_frames = jnp.concatenate(
        [key_rows[row_count - last_rows :], value_rows[row_count - last_rows :]], axis=-1
    )
    before = from_behind(last_frames, "tm", 1)
    all_lists = gather_lists(recalled, blocks)
    targets = jnp.arange(blocks * frame_count, dtype=jnp.int32)
    wanted = jnp.any(recalled.reshape(-1, 1) == targets[None, :], axis=0).reshape(
        blocks, frame_count
    )
    slot_rank = jnp.cumsum(wanted.astype(jnp.int32), axis=1) - 1
    mem_ok = recalled >= 0
    slot_frame = jnp.where(
        wanted[:, None, :] & (slot_rank[:, None, :] == jnp.arange(CAP, dtype=jnp.int32)[:, None]),
        targets.reshape(blocks, 1, frame_count) + 1,
        0,
    ).sum(axis=-1).reshape(-1) - 1
    slot_ok = jnp.any(
        mem_ok[:, :, None] & (recalled[:, :, None] == slot_frame[None, None, :]), axis=1
    )
    pool_frame = first_frame + jnp.concatenate(
        [jnp.arange(frame_count, dtype=jnp.int32), jnp.arange(-BAND, 0, dtype=jnp.int32)]
    )
    ahead = (first_frame + jnp.arange(frame_count, dtype=jnp.int32))[:, None] - pool_frame[None, :]
    band_ok = (ahead >= 0) & (ahead <= BAND) & (pool_frame >= 0)[None, :]
    frame_ok = jnp.concatenate([band_ok, slot_ok], axis=1)
    bias = jnp.where(frame_ok, 0.0, masked_score).astype(jnp.float32)
    bias = jnp.repeat(jnp.repeat(bias, frame_tokens, axis=0), frame_tokens, axis=1)
    own_frames = first_frame + jnp.arange(frame_count, dtype=jnp.int32)
    requested = jnp.any(
        all_lists.reshape(blocks, frame_count * MEM, 1) == own_frames[None, None, :], axis=1
    )
    asked_rank = jnp.cumsum(requested.astype(jnp.int32), axis=1) - 1
    picker = requested[:, None, :] & (
        asked_rank[:, None, :] == jnp.arange(CAP, dtype=jnp.int32)[None, :, None]
    )
    picker = picker.astype(jnp.bfloat16)
    out_keys = jnp.einsum(
        "bcp,pz->bcz", picker, key_rows.reshape(frame_count, -1), preferred_element_type=jnp.float32
    )
    out_values = jnp.einsum(
        "bcp,pz->bcz",
        picker,
        value_rows.reshape(frame_count, -1),
        preferred_element_type=jnp.float32,
    )
    piece_shape = (blocks, CAP, frame_tokens, inner_width)
    outgoing = jnp.concatenate(
        [
            out_keys.astype(jnp.bfloat16).reshape(piece_shape),
            out_values.astype(jnp.bfloat16).reshape(piece_shape),
        ],
        axis=-1,
    )
    incoming = lax.all_to_all(outgoing, "tm", split_axis=0, concat_axis=0, tiled=True)
    incoming, before, input_pair, grad_pair = lax.optimization_barrier(
        (incoming, before, input_pair, grad_pair)
    )
    slot_rows = incoming.reshape(blocks * CAP * frame_tokens, 2 * inner_width)
    (
        heads_rows, query_rows, own_keys, own_values, rim_keys, rim_values, slot_keys, slot_values
    ) = attend(queries, grad_heads, key_rows, value_rows, before, slot_rows, bias)
    rim = jnp.concatenate([rim_keys, rim_values], axis=-1)
    passed = from_behind(rim, "tm", -1)
    slot_grad = jnp.concatenate([slot_keys, slot_values], axis=-1).reshape(piece_shape[:3] + (-1,))
    returned = lax.all_to_all(slot_grad, "tm", split_axis=0, concat_axis=0, tiled=True)
    rollouts = lax.axis_size("roll")
    query_keep, query_give = column_halves(query_rows)
    early = reduce_all(
        partial_halves(flat_input, input_pair, query_keep, from_pair(query_give))
        + partial_halves(heads_rows, from_pair(heads_rows), grad_keep, grad_pair),
        blocks, rollouts, 0,
    )
    returned, passed, early = lax.optimization_barrier((returned, passed, early))
    passed_full = jnp.pad(passed.astype(jnp.float32), ((row_count - last_rows, 0), (0, 0)))
    gathered_back = jnp.einsum(
        "bcp,bcz->pz", picker, returned.reshape(blocks, CAP, -1), preferred_element_type=jnp.float32
    )
    gathered_back = gathered_back.reshape(row_count, 2 * inner_width)
    grad_keys = (
        own_keys + passed_full[..., :inner_width] + gathered_back[..., :inner_width]
    ).astype(jnp.bfloat16)
    grad_values = (
        own_values + passed_full[..., inner_width:] + gathered_back[..., inner_width:]
    ).astype(jnp.bfloat16)
    grad_input = (
        dot_last(query_rows, w_query) + dot_last(grad_keys, w_key) + dot_last(grad_values, w_value)
    )
    grad_input = grad_input.astype(jnp.bfloat16).reshape(1, frame_count, frame_tokens, model_width)
    attended = jnp.dot(heads_rows, w_output, preferred_element_type=jnp.float32).astype(
        jnp.bfloat16
    )
    attended = attended.reshape(1, frame_count, frame_tokens, model_width)
    key_keep, key_give = column_halves(grad_keys)
    value_keep, value_give = column_halves(grad_values)
    late = reduce_all(
        partial_halves(flat_input, input_pair, key_keep, from_pair(key_give))
        + partial_halves(flat_input, input_pair, value_keep, from_pair(value_give)),
        blocks, rollouts, 1,
    )
    totals = [
        assembled(*pieces)
        for pieces in (early[:2], late[:2], late[2:], early[2:])
    ]
    return (attended, grad_input, totals[0], totals[1], totals[2], totals[3])


def solution(mesh):
    return jax.shard_map(
        local,
        mesh=mesh,
        in_specs=(
            P("roll", "tm", None, None),
            P("roll", "tm", None, None),
            P("roll", "tm", None),
            P(),
            P(),
            P(),
            P(),
        ),
        out_specs=(
            P("roll", "tm", None, None),
            P("roll", "tm", None, None),
            P("tm", None),
            P("tm", None),
            P("tm", None),
            P("tm", None),
        ),
        check_vma=False,
    )
```
